32 devices in a mesh: cfg: 2 (over y), space: 8 (over z, x), tm: 2 (over core).
Axes of the slice: x: 2, y: 2, z: 4, core: 2. Of those that a mesh axis runs over, the one named last changes fastest.
Arguments:
- eigvecs: bfloat16 [4, 2, 3, 1536, 256], P(('cfg', 'tm'), None, None, 'space'), parts along dimension 0, may hold values from -6 to 6
- momenta: int32 [3, 3], replicated, may hold values from -2 to 2, as said below
- pair_list: int32 [8, 2], P('tm'), may hold values from 0 to 1
- panels: bfloat16 [16, 2, 1024, 1024], P(('cfg', 'tm'), None, 'space'), parts along dimension 0, may hold values from -6 to 6
Outputs:
- dressed: bfloat16 [16, 3, 2, 1024, 1024], P(('cfg', 'tm'), None, None, 'space'), parts along dimension 0
The draws below stay inside these ranges and needn't reach their ends.
There are 2 independent parts, one for each index of `cfg`. The reference program is written for one: setup_inputs(seed, part) draws one part's arguments, and reference() takes and returns one part's arrays. A program takes and returns all parts, laid end to end along the dimension named above; an argument that names none is the same for every part. Nothing has to cross between parts.
Inputs may be any that keep to these rules, and one draw needn't show every extreme that they name: `momenta`: the first component of every momentum is nonzero.
All inputs are finite; a program needn't handle non-finite values.
Results may differ from the reference program's by a relative error of at most 0.0075.
Values may be sent and summed in bfloat16 or wider, within the bound.
A program may use at most 64 MiB of HBM per device.

```python
import math
import jax
import jax.numpy as jnp
from jax import lax

LX = 64
NEV = 256
NSPIN = 4
NCOL = 3
NMOM = 3
T_WIN = 2
SITES = 1536
NPAIR = 8


def draw_momenta(key, part):
    key_mag = jax.random.fold_in(key, 11)
    key_sign = jax.random.fold_in(key, 12)
    key_rest = jax.random.fold_in(key, 13)
    magnitude = jax.random.randint(key_mag, (NMOM, 1), 1, 3)
    sign_part = jax.random.randint(key_sign, (NMOM, 1), 0, 2) * 2 - 1
    others = jax.random.randint(key_rest, (NMOM, 2), -2, 3)
    return jnp.concatenate([magnitude * sign_part, others], 1).astype(jnp.int32)


def place_ends(entries, key, smallest, top_value):
    extent = entries.shape
    index_at = [jax.random.randint(jax.random.fold_in(key, axis), (), 0, extent[axis]) for axis in range(len(extent))]
    entries = entries.at[tuple(index_at)].set(smallest)
    longest = extent.index(max(extent))
    index_at[longest] = (index_at[longest] + 1) % extent[longest]
    return entries.at[tuple(index_at)].set(top_value)


def block_levels(rng, extent, cuts, least, top_value):
    loudness, own = 1.0, jax.random.fold_in(rng, 6)
    for dim, shards_of in cuts:
        steps = jnp.exp(jax.random.uniform(jax.random.fold_in(own, dim), (shards_of,), jnp.float32, least / len(cuts), top_value / len(cuts)))
        loudness = loudness * jnp.repeat(steps, extent[dim] // shards_of).reshape([-1 if axis == dim else 1 for axis in range(len(extent))])
    return loudness


def scatter_about(stream_key, extent, width, limit, pieces=(), kind=jnp.bfloat16):
    factor_of = block_levels(stream_key, extent, pieces, -0.22, 0.18) if pieces else 1.0
    drawn = jax.random.normal(stream_key, extent, jnp.float32) * width * factor_of
    return jnp.minimum(jnp.maximum(drawn, -limit), limit).astype(kind)


def setup_inputs(seed: int = 0, part: int = 0) -> dict:
    key_list = jax.random.split(jax.random.key(seed), 5)
    own_keys = jax.random.split(jax.random.fold_in(key_list[4], part), 5)
    return {
        "eigvecs": scatter_about(own_keys[0], (T_WIN, 2, NCOL, SITES, NEV), 1.0, 6.0, ((0, 2), (3, 8))),
        "momenta": draw_momenta(jax.random.fold_in(key_list[4], 71), part),
        "pair_list": place_ends(jax.random.randint(key_list[2], (NPAIR, 2), 0, T_WIN), jax.random.fold_in(key_list[2], 1), 0, T_WIN - 1).astype(jnp.int32),
        "panels": scatter_about(own_keys[3], (NPAIR, 2, NSPIN * NEV, NSPIN * NEV), 1.0, 6.0, ((0, 2), (2, 8))),
    }


def phase_table(momenta, site_index):
    xpos = site_index % LX
    ypos = site_index // LX % LX
    zpos = site_index // (LX * LX)
    wave = momenta[:, 0:1] * xpos[None, :] + momenta[:, 1:2] * ypos[None, :] + momenta[:, 2:3] * zpos[None, :]
    wave = jnp.mod(wave, LX)
    angle = wave.astype(jnp.float32) * jnp.float32(2.0 * math.pi / LX)
    return (jnp.cos(angle), jnp.sin(angle))

def phased_block(cosine, sine_part, real_part, imag_part):
    cos_col = cosine[:, None]
    sin_col = sine_part[:, None]
    wave_re = cos_col * real_part + sin_col * imag_part
    wave_im = cos_col * imag_part - sin_col * real_part
    upper = jnp.concatenate([wave_re, wave_im], -1)
    lower = jnp.concatenate([wave_im, -wave_re], -1)
    return jnp.stack([upper, lower], -4).astype(jnp.bfloat16)

def reference(eigvecs, momenta, pair_list, panels):
    site_index = jnp.arange(SITES, dtype=jnp.int32)
    cosine, sine_part = phase_table(momenta, site_index)
    factor = 1.0 / math.sqrt(6.0 * SITES * NEV)
    fields = []
    for slot in range(T_WIN):
        block = eigvecs[slot].astype(jnp.float32)
        per_moment = []
        for moment in range(NMOM):
            phased = phased_block(cosine[moment], sine_part[moment], block[0], block[1])
            gram_sum = jnp.einsum('rcsk,rcsl->kl', block, phased.astype(jnp.float32), precision=lax.Precision.HIGHEST)
            per_moment.append((factor * gram_sum).astype(jnp.bfloat16))
        fields.append(jnp.stack(per_moment, 0))
    meson_fields = jnp.stack(fields, 0)
    results = []
    for pair in range(NPAIR):
        source_fields = meson_fields[pair_list[pair, 0]].reshape(NMOM, NEV, 2, NEV).astype(jnp.float32)
        sink_fields = meson_fields[pair_list[pair, 1]].reshape(NMOM, NEV, 2, NEV).astype(jnp.float32)
        panel_parts = panels[pair].reshape(2, NSPIN * NEV, NSPIN, NEV).astype(jnp.float32)
        panel_re = panel_parts[0]
        panel_im = panel_parts[1]
        panel_mix = jnp.stack([jnp.stack([panel_re, panel_im], 0), jnp.stack([panel_im, -panel_re], 0)], 0)
        right_dressed = jnp.einsum('orxbk,mlrk->moxbl', panel_mix, source_fields, precision=lax.Precision.HIGHEST)
        right_dressed = right_dressed.astype(jnp.bfloat16).astype(jnp.float32)
        right_dressed = right_dressed.reshape(NMOM, 2, NSPIN, NEV, NSPIN * NEV)
        right_re = right_dressed[:, 0]
        right_im = right_dressed[:, 1]
        mixed_parts = jnp.stack([jnp.stack([right_re, -right_im], 1), jnp.stack([right_im, right_re], 1)], 1)
        dressed_pair = jnp.einsum('morajc,mkrj->mocak', mixed_parts, sink_fields, precision=lax.Precision.HIGHEST)
        results.append(dressed_pair.reshape(NMOM, 2, NSPIN * NEV, NSPIN * NEV).astype(jnp.bfloat16))
    return jnp.stack(results, 0)
```

```python
import functools
import math

import jax
import jax.numpy as jnp
from jax import lax
from jax.experimental import pallas as pl
from jax.experimental.pallas import tpu as pltpu
from jax.sharding import PartitionSpec as P

LX = 64
MESH = pl.DeviceIdType.MESH


def phase_table(momenta, first_site, slab_sites):
    site_index = first_site + jnp.arange(slab_sites, dtype=jnp.int32)
    xpos = site_index % LX
    ypos = site_index // LX % LX
    zpos = site_index // (LX * LX)
    wave = (
        momenta[:, 0:1] * xpos[None, :]
        + momenta[:, 1:2] * ypos[None, :]
        + momenta[:, 2:3] * zpos[None, :]
    )
    wave = jnp.mod(wave, LX)
    angle = wave.astype(jnp.float32) * jnp.float32(2.0 * math.pi / LX)
    return jnp.cos(angle), jnp.sin(angle)


def exchange_kernel(
    factor, blocks, eig, trig, pan, tau, mes,
    stack, wave, gram, part, got_half, half32, half16, got_piece,
    s_half, r_half, s_piece, r_piece, s_field, r_field, s_swap, r_swap,
    s_core, r_core, s_pan, r_pan, s_own, r_own, s_fwd, r_fwd, s_loc,
):
    space = lax.axis_index("space")
    core = lax.axis_index("tm")
    block = space // 2
    side = space % 2
    other_side = block * 2 + (1 - side)
    pairs, _, rows, _ = pan.shape
    moms, vectors, _ = gram.shape
    colors, sites = eig.shape[2], eig.shape[3]
    hrows = vectors // 2
    prows = hrows // blocks

    def peer(step):
        return lax.rem(block + step, blocks)

    def sender(step):
        return lax.rem(block + blocks - step, blocks)

    def at(index):
        return {"space": index}

    barrier = pltpu.get_barrier_semaphore()
    for step in range(1, blocks):
        pl.semaphore_signal(
            barrier, inc=1, device_id=at(peer(step) * 2 + side), device_id_type=MESH
        )
    pl.semaphore_signal(barrier, inc=1, device_id=at(other_side), device_id_type=MESH)
    pl.semaphore_signal(barrier, inc=1, device_id={"tm": 1 - core}, device_id_type=MESH)
    pl.semaphore_wait(barrier, blocks + 1)

    def remote(src, dst, send, recv, device):
        return pltpu.make_async_remote_copy(
            src_ref=src, dst_ref=dst, send_sem=send, recv_sem=recv,
            device_id=device, device_id_type=MESH,
        )

    def tau_rows(owner):
        return pl.ds(pl.multiple_of(owner * rows, rows), rows)

    def pan_cols(index):
        return pl.ds(pl.multiple_of(index * vectors, vectors), vectors)

    along = [
        [
            remote(
                pan.at[p, :, :, pan_cols(peer(step))], tau.at[p, :, tau_rows(space), :],
                s_pan.at[p, step - 1], r_pan.at[p, step - 1], at(peer(step) * 2 + side),
            )
            for step in range(1, blocks)
        ]
        for p in range(pairs)
    ]
    own = [
        remote(
            pan.at[p, :, :, pan_cols(block)], tau.at[p, :, tau_rows(space), :],
            s_own.at[p], r_own.at[p], at(other_side),
        )
        for p in range(pairs)
    ]
    keep = [
        pltpu.make_async_copy(
            pan.at[p, :, :, pan_cols(block)], tau.at[p, :, tau_rows(space), :], s_loc.at[p]
        )
        for p in range(pairs)
    ]
    forward = [
        [
            remote(
                tau.at[p, :, tau_rows(sender(step) * 2 + side), :],
                tau.at[p, :, tau_rows(sender(step) * 2 + side), :],
                s_fwd.at[p, step - 1], r_fwd.at[p, step - 1], at(other_side),
            )
            for step in range(1, blocks)
        ]
        for p in range(pairs)
    ]
    my_half = pl.ds(pl.multiple_of(side * hrows, hrows), hrows)
    far_half = pl.ds(pl.multiple_of((1 - side) * hrows, hrows), hrows)
    my_piece = pl.ds(pl.multiple_of(side * hrows + block * prows, prows), prows)
    halves = [
        remote(part.at[m, far_half, :], got_half.at[m], s_half.at[m], r_half.at[m], at(other_side))
        for m in range(moms)
    ]
    pieces = [
        [
            remote(
                half16.at[m, pl.ds(pl.multiple_of(peer(step) * prows, prows), prows), :],
                got_piece.at[step - 1, m],
                s_piece.at[m, step - 1], r_piece.at[m, step - 1], at(peer(step) * 2 + side),
            )
            for step in range(1, blocks)
        ]
        for m in range(moms)
    ]
    fields = [
        [
            remote(
                mes.at[core, m, my_piece, :], mes.at[core, m, my_piece, :],
                s_field.at[m, step - 1], r_field.at[m, step - 1], at(peer(step) * 2 + side),
            )
            for step in range(1, blocks)
        ]
        for m in range(moms)
    ]
    swaps = [
        remote(
            mes.at[core, m, my_half, :], mes.at[core, m, my_half, :],
            s_swap.at[m], r_swap.at[m], at(other_side),
        )
        for m in range(moms)
    ]
    cores = [
        [
            remote(
                mes.at[core, m, which, :], mes.at[core, m, which, :],
                s_core.at[m, i], r_core.at[m, i], {"tm": 1 - core},
            )
            for i, which in enumerate((my_half, far_half))
        ]
        for m in range(moms)
    ]

    def send_along(p):
        for copy in along[p]:
            copy.start()

    def pass_on(p):
        for step in range(blocks - 1):
            along[p][step].wait_recv()
            forward[p][step].start()

    send_along(0)
    own[0].start()
    for copy in keep:
        copy.start()

    for color in range(colors):
        for r in range(2):
            stack[pl.ds((r * colors + color) * sites, sites), :] = eig[0, r, color]
    for m in range(moms):
        cos_col = trig[:, m : m + 1]
        sin_col = trig[:, moms + m : moms + m + 1]
        for color in range(colors):
            real_part = eig[0, 0, color].astype(jnp.float32)
            imag_part = eig[0, 1, color].astype(jnp.float32)
            wave_re = (cos_col * real_part + sin_col * imag_part).astype(jnp.bfloat16)
            wave_im = (cos_col * imag_part - sin_col * real_part).astype(jnp.bfloat16)
            upper = pl.ds(color * sites, sites)
            lower = pl.ds((colors + color) * sites, sites)
            wave[upper, :vectors] = wave_re
            wave[upper, vectors:] = wave_im
            wave[lower, :vectors] = wave_im
            wave[lower, vectors:] = -wave_re
        total = factor * lax.dot_general(
            stack[...], wave[...], (((0,), (0,)), ((), ())), preferred_element_type=jnp.float32
        )
        gram[m] = total
        part[m] = total.astype(jnp.bfloat16)
        halves[m].start()

    for m in range(moms):
        halves[m].wait_recv()
        value = gram[m, my_half, :] + got_half[m].astype(jnp.float32)
        half32[m] = value
        half16[m] = value.astype(jnp.bfloat16)
        for copy in pieces[m]:
            copy.start()
    if pairs > 1:
        send_along(1)
    for p in range(1, pairs):
        own[p].start()
    pass_on(0)

    for m in range(moms):
        value = half32[m, pl.ds(pl.multiple_of(block * prows, prows), prows), :]
        for step in range(blocks - 1):
            pieces[m][step].wait_recv()
            value = value + got_piece[step, m].astype(jnp.float32)
        mes[core, m, my_piece, :] = value.astype(jnp.bfloat16)
        for copy in fields[m]:
            copy.start()
    for p in range(2, pairs):
        send_along(p)
    if pairs > 1:
        pass_on(1)
    for m in range(moms):
        for copy in fields[m]:
            copy.wait_recv()
        swaps[m].start()
        cores[m][0].start()
    if pairs > 2:
        pass_on(2)
    for m in range(moms):
        swaps[m].wait_recv()
        cores[m][1].start()
    for p in range(3, pairs):
        pass_on(p)

    for m in range(moms):
        halves[m].wait_send()
        swaps[m].wait_send()
        for copy in pieces[m] + fields[m]:
            copy.wait_send()
        for copy in cores[m]:
            copy.wait()
    for p in range(pairs):
        keep[p].wait()
        own[p].wait()
        for copy in along[p]:
            copy.wait_send()
        for copy in forward[p]:
            copy.wait()


def exchange(eigvecs, trig, panels, spins):
    pairs, _, rows, width = panels.shape
    _, _, colors, sites, vectors = eigvecs.shape
    moms = trig.shape[1] // 2
    space_count = lax.axis_size("space")
    slices = lax.axis_size("tm")
    factor = 1.0 / math.sqrt(6.0 * sites * space_count * vectors)
    hrows = vectors // 2
    prows = hrows // spins
    bf16, f32 = jnp.bfloat16, jnp.float32
    dma = pltpu.SemaphoreType.DMA
    others = spins - 1
    vmem = pl.BlockSpec(memory_space=pltpu.VMEM)
    return pl.pallas_call(
        functools.partial(exchange_kernel, factor, spins),
        out_shape=(
            jax.ShapeDtypeStruct((pairs, 2, rows * space_count, vectors), bf16),
            jax.ShapeDtypeStruct((slices, moms, vectors, 2 * vectors), bf16),
        ),
        in_specs=[vmem] * 3,
        out_specs=(pl.BlockSpec(memory_space=pl.ANY), vmem),
        scratch_shapes=[
            pltpu.VMEM((2 * colors * sites, vectors), bf16),
            pltpu.VMEM((2 * colors * sites, 2 * vectors), bf16),
            pltpu.VMEM((moms, vectors, 2 * vectors), f32),
            pltpu.VMEM((moms, vectors, 2 * vectors), bf16),
            pltpu.VMEM((moms, hrows, 2 * vectors), bf16),
            pltpu.VMEM((moms, hrows, 2 * vectors), f32),
            pltpu.VMEM((moms, hrows, 2 * vectors), bf16),
            pltpu.VMEM((others, moms, prows, 2 * vectors), bf16),
            dma((moms,)), dma((moms,)),
            dma((moms, others)), dma((moms, others)),
            dma((moms, others)), dma((moms, others)),
            dma((moms,)), dma((moms,)),
            dma((moms, 2)), dma((moms, 2)),
            dma((pairs, others)), dma((pairs, others)),
            dma((pairs,)), dma((pairs,)),
            dma((pairs, others)), dma((pairs, others)),
            dma((pairs,)),
        ],
        compiler_params=pltpu.CompilerParams(
            collective_id=0, has_side_effects=True, vmem_limit_bytes=40 << 20
        ),
        name="exchange",
    )(eigvecs, trig, panels)


def multiply_kernel(spins, list_ref, side_ref, tau, mes, out, left, right, sink):
    pair = pl.program_id(0)
    source = list_ref[pair, 0]
    target = list_ref[pair, 1]
    moms, vectors = mes.shape[1], mes.shape[2]
    cols = out.shape[3]
    own = pl.ds(pl.multiple_of(side_ref[0] * cols, cols), cols)
    for m in range(moms):
        real_part = mes[source, m, own, :vectors]
        imag_part = mes[source, m, own, vectors:]
        left[pl.ds(2 * m * cols, cols), :vectors] = real_part
        left[pl.ds(2 * m * cols, cols), vectors:] = imag_part
        left[pl.ds((2 * m + 1) * cols, cols), :vectors] = -imag_part
        left[pl.ds((2 * m + 1) * cols, cols), vectors:] = real_part
    turned = (((1,), (1,)), ((), ()))
    for spin in range(spins):
        rows = pl.ds(spin * vectors, vectors)
        value = lax.dot_general(
            left[:, :vectors], tau[0, 0, rows, :], turned, preferred_element_type=jnp.float32
        ) + lax.dot_general(
            left[:, vectors:], tau[0, 1, rows, :], turned, preferred_element_type=jnp.float32
        )
        value = value.astype(jnp.bfloat16)
        for m in range(moms):
            for o in range(2):
                right[m, pl.ds(spin * cols, cols), o * vectors : (o + 1) * vectors] = value[
                    (2 * m + o) * cols : (2 * m + o + 1) * cols
                ]
    for m in range(moms):
        real_part = mes[target, m, :, :vectors]
        imag_part = mes[target, m, :, vectors:]
        sink[:vectors, :vectors] = real_part
        sink[:vectors, vectors:] = -imag_part
        sink[vectors:, :vectors] = imag_part
        sink[vectors:, vectors:] = real_part
        value = lax.dot_general(
            right[m], sink[...], turned, preferred_element_type=jnp.float32
        ).astype(jnp.bfloat16)
        for spin in range(spins):
            for o in range(2):
                out[0, m, o, :, pl.ds(spin * vectors, vectors)] = value[
                    spin * cols : (spin + 1) * cols, o * vectors : (o + 1) * vectors
                ]


def multiply(pair_list, side, tau, mes, spins):
    pairs, _, width, vectors = tau.shape
    slices, moms = mes.shape[:2]
    cols = width // lax.axis_size("space")
    bf16 = jnp.bfloat16
    return pl.pallas_call(
        functools.partial(multiply_kernel, spins),
        out_shape=jax.ShapeDtypeStruct((pairs, moms, 2, cols, width), bf16),
        grid_spec=pltpu.PrefetchScalarGridSpec(
            num_scalar_prefetch=2,
            grid=(pairs,),
            in_specs=[
                pl.BlockSpec((1, 2, width, vectors), lambda p, *_: (p, 0, 0, 0)),
                pl.BlockSpec(mes.shape, lambda p, *_: (0, 0, 0, 0)),
            ],
            out_specs=pl.BlockSpec((1, moms, 2, cols, width), lambda p, *_: (p, 0, 0, 0, 0)),
            scratch_shapes=[
                pltpu.VMEM((2 * moms * cols, 2 * vectors), bf16),
                pltpu.VMEM((moms, spins * cols, 2 * vectors), bf16),
                pltpu.VMEM((2 * vectors, 2 * vectors), bf16),
            ],
        ),
        compiler_params=pltpu.CompilerParams(vmem_limit_bytes=40 << 20),
        name="multiply",
    )(pair_list, side, tau, mes)


def local_kernels(eigvecs, momenta, pair_list, panels):
    slab_sites, vectors = eigvecs.shape[3:]
    spins = panels.shape[3] // vectors
    space = lax.axis_index("space")
    cosine, sine = phase_table(momenta, space * slab_sites, slab_sites)
    trig = jnp.concatenate([cosine, sine], 0).T
    tau, mes = exchange(eigvecs, trig, panels, spins)
    side = jnp.reshape(space % 2, (1,)).astype(jnp.int32)
    return multiply(pair_list, side, tau, mes, spins)


def phased_block(cosine, sine_part, real_part, imag_part):
    cos_col = cosine[:, None]
    sin_col = sine_part[:, None]
    wave_re = cos_col * real_part + sin_col * imag_part
    wave_im = cos_col * imag_part - sin_col * real_part
    upper = jnp.concatenate([wave_re, wave_im], -1)
    lower = jnp.concatenate([wave_im, -wave_re], -1)
    return jnp.stack([upper, lower], -4).astype(jnp.bfloat16)


def local_general(eigvecs, momenta, pair_list, panels):
    slice_count, _, colors, slab_sites, vectors = eigvecs.shape
    mom_count = momenta.shape[0]
    space_count = lax.axis_size("space")
    cosine, sine_part = phase_table(momenta, lax.axis_index("space") * slab_sites, slab_sites)
    factor = 1.0 / math.sqrt(6.0 * slab_sites * space_count * vectors)
    real_part = eigvecs[:, 0].astype(jnp.float32)
    imag_part = eigvecs[:, 1].astype(jnp.float32)
    phased_all = jnp.concatenate(
        [
            phased_block(cosine[moment], sine_part[moment], real_part, imag_part)
            for moment in range(mom_count)
        ],
        -1,
    )
    phased_all = phased_all.reshape(slice_count, 2, colors, slab_sites, mom_count, 2 * vectors)
    gram_local = jnp.einsum(
        "trcsk,trcsml->tmkl", eigvecs, phased_all, preferred_element_type=jnp.float32
    )
    gram_local = factor * gram_local
    summed = lax.psum(gram_local, "space")
    own_fields = summed.astype(jnp.bfloat16)
    meson_fields = lax.all_gather(own_fields, "tm", axis=0, tiled=True)
    pair_count = pair_list.shape[0]
    panel_rows = panels.shape[2]
    panel_width = panels.shape[3]
    spins = panel_width // vectors
    source_fields = jnp.take(meson_fields, pair_list[:, 0], axis=0).reshape(
        pair_count, mom_count, vectors, 2, vectors
    )
    sink_fields = jnp.take(meson_fields, pair_list[:, 1], axis=0).reshape(
        pair_count, mom_count, vectors, 2, vectors
    )
    panel_parts = panels.reshape(pair_count, 2, panel_rows, spins, vectors)
    panel_re = panel_parts[:, 0]
    panel_im = panel_parts[:, 1]
    panel_mix = jnp.stack(
        [jnp.stack([panel_re, panel_im], 1), jnp.stack([panel_im, -panel_re], 1)], 1
    )
    right_dressed = jnp.einsum(
        "porxbk,pmlrk->pmoxbl", panel_mix, source_fields, preferred_element_type=jnp.float32
    )
    right_dressed = right_dressed.astype(jnp.bfloat16).reshape(
        pair_count * mom_count, 2, panel_rows, panel_width
    )
    turned = lax.all_to_all(right_dressed, "space", split_axis=3, concat_axis=2, tiled=True)
    column_count = turned.shape[3]
    turned = turned.reshape(pair_count, mom_count, 2, spins, vectors, column_count)
    turned_re = turned[:, :, 0]
    turned_im = turned[:, :, 1]
    mixed_parts = jnp.stack(
        [jnp.stack([turned_re, -turned_im], 2), jnp.stack([turned_im, turned_re], 2)], 2
    )
    dressed = jnp.einsum(
        "pmorajc,pmkrj->pmocak", mixed_parts, sink_fields, preferred_element_type=jnp.float32
    )
    return dressed.reshape(pair_count, mom_count, 2, column_count, panel_width).astype(jnp.bfloat16)


def local(eigvecs, momenta, pair_list, panels):
    slices, _, _, _, vectors = eigvecs.shape
    spins = panels.shape[3] // vectors
    fits = (
        slices == 1
        and lax.axis_size("tm") == 2
        and lax.axis_size("space") == 2 * spins
        and spins > 1
        and panels.shape[2] * 2 == vectors
        and panels.shape[2] % 128 == 0
        and (vectors // 2) % (16 * spins) == 0
    )
    return (local_kernels if fits else local_general)(eigvecs, momenta, pair_list, panels)


def solution(mesh):
    placed = (
        P(("cfg", "tm"), None, None, "space", None),
        P(),
        P("tm", None),
        P(("cfg", "tm"), None, "space", None),
    )
    return jax.shard_map(
        local,
        mesh=mesh,
        in_specs=placed,
        out_specs=P(("cfg", "tm"), None, None, "space", None),
        check_vma=False,
    )
```

```python
import functools
import math

import jax
import jax.numpy as jnp
from jax import lax
from jax.experimental import pallas as pl
from jax.experimental.pallas import tpu as pltpu
from jax.sharding import PartitionSpec as P

LX = 64
MESH = pl.DeviceIdType.MESH


def phase_table(momenta, first_site, slab_sites):
    site_index = first_site + jnp.arange(slab_sites, dtype=jnp.int32)
    xpos = site_index % LX
    ypos = site_index // LX % LX
    zpos = site_index // (LX * LX)
    wave = (
        momenta[:, 0:1] * xpos[None, :]
        + momenta[:, 1:2] * ypos[None, :]
        + momenta[:, 2:3] * zpos[None, :]
    )
    wave = jnp.mod(wave, LX)
    angle = wave.astype(jnp.float32) * jnp.float32(2.0 * math.pi / LX)
    return jnp.cos(angle), jnp.sin(angle)


def exchange_kernel(
    factor, blocks, momenta, pair_list, eig_hbm, pan, out,
    tau, mes, left, right, sink, made, eig, stack, wave, gram, part, got_half, half32, half16, got_piece,
    s_half, r_half, s_piece, r_piece, s_field, r_field, s_swap, r_swap,
    s_core, r_core, s_pan, r_pan, s_own, r_own, s_fwd, r_fwd, s_loc, s_eig, s_out,
):
    space = lax.axis_index("space")
    core = lax.axis_index("tm")
    block = space // 2
    side = space % 2
    other_side = block * 2 + (1 - side)
    pairs, _, rows, _ = pan.shape
    moms, vectors, _ = gram.shape
    colors, sites = eig.shape[1], eig.shape[2]
    hrows = vectors // 2
    prows = hrows // blocks

    fetch = pltpu.make_async_copy(eig_hbm.at[0], eig, s_eig)
    fetch.start()

    def peer(step):
        index, bit = block, 1
        while bit < blocks:
            if (blocks - step) & bit:
                index = index + bit * (1 - 2 * ((block // bit) % 2))
            bit *= 2
        return index

    sender = peer

    def at(index):
        return {"space": index}

    barrier = pltpu.get_barrier_semaphore()
    for step in range(1, blocks):
        pl.semaphore_signal(
            barrier, inc=1, device_id=at(peer(step) * 2 + side), device_id_type=MESH
        )
    pl.semaphore_signal(barrier, inc=1, device_id=at(other_side), device_id_type=MESH)
    pl.semaphore_signal(barrier, inc=1, device_id={"tm": 1 - core}, device_id_type=MESH)
    pl.semaphore_wait(barrier, blocks + 1)

    def remote(src, dst, send, recv, device):
        return pltpu.make_async_remote_copy(
            src_ref=src, dst_ref=dst, send_sem=send, recv_sem=recv,
            device_id=device, device_id_type=MESH,
        )

    def tau_rows(owner):
        return pl.ds(pl.multiple_of(owner * rows, rows), rows)

    def pan_cols(index):
        return pl.ds(pl.multiple_of(index * vectors, vectors), vectors)

    along = [
        [
            remote(
                pan.at[p, :, :, pan_cols(peer(step))], tau.at[p, :, tau_rows(space), :],
                s_pan.at[p, step - 1], r_pan.at[p, step - 1], at(peer(step) * 2 + side),
            )
            for step in range(1, blocks)
        ]
        for p in range(pairs)
    ]
    own = [
        remote(
            pan.at[p, :, :, pan_cols(block)], tau.at[p, :, tau_rows(space), :],
            s_own.at[p], r_own.at[p], at(other_side),
        )
        for p in range(pairs)
    ]
    keep = [
        pltpu.make_async_copy(
            pan.at[p, :, :, pan_cols(block)], tau.at[p, :, tau_rows(space), :], s_loc.at[p]
        )
        for p in range(pairs)
    ]
    forward = [
        [
            remote(
                tau.at[p, :, tau_rows(sender(step) * 2 + side), :],
                tau.at[p, :, tau_rows(sender(step) * 2 + side), :],
                s_fwd.at[p, step - 1], r_fwd.at[p, step - 1], at(other_side),
            )
            for step in range(1, blocks)
        ]
        for p in range(pairs)
    ]
    my_half = pl.ds(pl.multiple_of(side * hrows, hrows), hrows)
    far_half = pl.ds(pl.multiple_of((1 - side) * hrows, hrows), hrows)
    my_piece = pl.ds(pl.multiple_of(side * hrows + block * prows, prows), prows)
    halves = [
        remote(part.at[m, far_half, :], got_half.at[m], s_half.at[m], r_half.at[m], at(other_side))
        for m in range(moms)
    ]
    pieces = [
        [
            remote(
                half16.at[m, pl.ds(pl.multiple_of(peer(step) * prows, prows), prows), :],
                got_piece.at[step - 1, m],
                s_piece.at[m, step - 1], r_piece.at[m, step - 1], at(peer(step) * 2 + side),
            )
            for step in range(1, blocks)
        ]
        for m in range(moms)
    ]
    fields = [
        [
            remote(
                mes.at[core, m, my_piece, :], mes.at[core, m, my_piece, :],
                s_field.at[m, step - 1], r_field.at[m, step - 1], at(peer(step) * 2 + side),
            )
            for step in range(1, blocks)
        ]
        for m in range(moms)
    ]
    swaps = [
        remote(
            mes.at[core, m, my_half, :], mes.at[core, m, my_half, :],
            s_swap.at[m], r_swap.at[m], at(other_side),
        )
        for m in range(moms)
    ]
    cores = [
        [
            remote(
                mes.at[core, m, which, :], mes.at[core, m, which, :],
                s_core.at[m, i], r_core.at[m, i], {"tm": 1 - core},
            )
            for i, which in enumerate((my_half, far_half))
        ]
        for m in range(moms)
    ]

    def send_along(p):
        for copy in along[p]:
            copy.start()

    def pass_on(p):
        for step in range(blocks - 1):
            along[p][step].wait_recv()
            forward[p][step].start()

    put = [pltpu.make_async_copy(made.at[p], out.at[p], s_out.at[p]) for p in range(pairs)]
    turned = (((1,), (1,)), ((), ()))

    def dress(p):
        from_first = pair_list[0, p] == 0
        to_first = pair_list[1, p] == 0
        for m in range(moms):
            field = jnp.where(from_first, mes[0, m, my_half, :], mes[1, m, my_half, :])
            real_part = field[:, :vectors]
            imag_part = field[:, vectors:]
            left[pl.ds(2 * m * hrows, hrows), :vectors] = real_part
            left[pl.ds(2 * m * hrows, hrows), vectors:] = imag_part
            left[pl.ds((2 * m + 1) * hrows, hrows), :vectors] = -imag_part
            left[pl.ds((2 * m + 1) * hrows, hrows), vectors:] = real_part
        for spin in range(blocks):
            spin_rows = pl.ds(spin * vectors, vectors)
            value = lax.dot_general(
                left[:, :vectors], tau[p, 0, spin_rows, :], turned,
                preferred_element_type=jnp.float32,
            ) + lax.dot_general(
                left[:, vectors:], tau[p, 1, spin_rows, :], turned,
                preferred_element_type=jnp.float32,
            )
            value = value.astype(jnp.bfloat16)
            for m in range(moms):
                for o in range(2):
                    right[m, pl.ds(spin * hrows, hrows), o * vectors : (o + 1) * vectors] = value[
                        (2 * m + o) * hrows : (2 * m + o + 1) * hrows
                    ]
        for m in range(moms):
            field = jnp.where(to_first, mes[0, m], mes[1, m])
            real_part = field[:, :vectors]
            imag_part = field[:, vectors:]
            sink[:vectors, :vectors] = real_part
            sink[:vectors, vectors:] = -imag_part
            sink[vectors:, :vectors] = imag_part
            sink[vectors:, vectors:] = real_part
            value = lax.dot_general(
                right[m], sink[...], turned, preferred_element_type=jnp.float32
            ).astype(jnp.bfloat16)
            for spin in range(blocks):
                for o in range(2):
                    made[p, m, o, :, pl.ds(spin * vectors, vectors)] = value[
                        spin * hrows : (spin + 1) * hrows, o * vectors : (o + 1) * vectors
                    ]
        put[p].start()

    def settle(p):
        keep[p].wait()
        own[p].wait_recv()
        for copy in forward[p]:
            copy.wait_recv()

    for p in range(min(2, pairs)):
        send_along(p)
    own[0].start()
    for copy in keep:
        copy.start()

    site = space * sites + lax.broadcasted_iota(jnp.int32, (sites, 128), 0)
    lane = lax.broadcasted_iota(jnp.int32, (sites, 128), 1)
    turn = jnp.zeros((sites, 128), jnp.int32)
    shift = LX.bit_length() - 1
    for m in range(moms):
        sum_m = (
            momenta[m, 0] * (site & (LX - 1))
            + momenta[m, 1] * (lax.shift_right_logical(site, shift) & (LX - 1))
            + momenta[m, 2] * lax.shift_right_logical(site, 2 * shift)
        )
        turn = jnp.where(lane == m, sum_m & (LX - 1), turn)
    angle = turn.astype(jnp.float32) * jnp.float32(2.0 * math.pi / LX)
    cosine = jnp.cos(angle)
    sine = jnp.sin(angle)
    fetch.wait()
    for color in range(colors):
        for r in range(2):
            stack[pl.ds((r * colors + color) * sites, sites), :] = eig[r, color]
    for m in range(moms):
        cos_col = cosine[:, m : m + 1]
        sin_col = sine[:, m : m + 1]
        for color in range(colors):
            real_part = eig[0, color].astype(jnp.float32)
            imag_part = eig[1, color].astype(jnp.float32)
            wave_re = (cos_col * real_part + sin_col * imag_part).astype(jnp.bfloat16)
            wave_im = (cos_col * imag_part - sin_col * real_part).astype(jnp.bfloat16)
            upper = pl.ds(color * sites, sites)
            lower = pl.ds((colors + color) * sites, sites)
            wave[upper, :vectors] = wave_re
            wave[upper, vectors:] = wave_im
            wave[lower, :vectors] = wave_im
            wave[lower, vectors:] = -wave_re
        total = factor * lax.dot_general(
            stack[...], wave[...], (((0,), (0,)), ((), ())), preferred_element_type=jnp.float32
        )
        gram[m] = total
        part[m] = total.astype(jnp.bfloat16)
        halves[m].start()

    for p in range(1, pairs):
        own[p].start()
    for m in range(moms):
        halves[m].wait_recv()
        value = gram[m, my_half, :] + got_half[m].astype(jnp.float32)
        half32[m] = value
        half16[m] = value.astype(jnp.bfloat16)
        for copy in pieces[m]:
            copy.start()
    for p in range(2, min(3, pairs)):
        send_along(p)
    pass_on(0)

    for m in range(moms):
        value = half32[m, pl.ds(pl.multiple_of(block * prows, prows), prows), :]
        for step in range(blocks - 1):
            pieces[m][step].wait_recv()
            value = value + got_piece[step, m].astype(jnp.float32)
        mes[core, m, my_piece, :] = value.astype(jnp.bfloat16)
        for copy in fields[m]:
            copy.start()
    for p in range(3, pairs):
        send_along(p)
    if pairs > 1:
        pass_on(1)
    for m in range(moms):
        for copy in fields[m]:
            copy.wait_recv()
        swaps[m].start()
        cores[m][0].start()
    if pairs > 2:
        pass_on(2)
    for m in range(moms):
        swaps[m].wait_recv()
        cores[m][1].start()
    for m in range(moms):
        for copy in cores[m]:
            copy.wait_recv()
    settle(0)
    dress(0)
    for p in range(3, pairs):
        pass_on(p)
    for p in range(1, pairs):
        settle(p)
        dress(p)

    for m in range(moms):
        halves[m].wait_send()
        swaps[m].wait_send()
        for copy in pieces[m] + fields[m] + cores[m]:
            copy.wait_send()
    for p in range(pairs):
        own[p].wait_send()
        for copy in along[p] + forward[p]:
            copy.wait_send()
        put[p].wait()


def exchange(eigvecs, momenta, pair_list, panels, spins):
    pairs, _, rows, width = panels.shape
    _, _, colors, sites, vectors = eigvecs.shape
    moms = momenta.shape[0]
    space_count = lax.axis_size("space")
    slices = lax.axis_size("tm")
    factor = 1.0 / math.sqrt(6.0 * sites * space_count * vectors)
    hrows = vectors // 2
    prows = hrows // spins
    bf16, f32 = jnp.bfloat16, jnp.float32
    dma = pltpu.SemaphoreType.DMA
    others = spins - 1
    smem = pl.BlockSpec(memory_space=pltpu.SMEM)
    hbm = pl.BlockSpec(memory_space=pl.ANY)
    return pl.pallas_call(
        functools.partial(exchange_kernel, factor, spins),
        out_shape=jax.ShapeDtypeStruct((pairs, moms, 2, rows, width), bf16),
        in_specs=[smem, smem, hbm, hbm],
        out_specs=hbm,
        scratch_shapes=[
            pltpu.VMEM((pairs, 2, rows * space_count, vectors), bf16),
            pltpu.VMEM((slices, moms, vectors, 2 * vectors), bf16),
            pltpu.VMEM((2 * moms * hrows, 2 * vectors), bf16),
            pltpu.VMEM((moms, spins * hrows, 2 * vectors), bf16),
            pltpu.VMEM((2 * vectors, 2 * vectors), bf16),
            pltpu.VMEM((pairs, moms, 2, rows, width), bf16),
            pltpu.VMEM((2, colors, sites, vectors), bf16),
            pltpu.VMEM((2 * colors * sites, vectors), bf16),
            pltpu.VMEM((2 * colors * sites, 2 * vectors), bf16),
            pltpu.VMEM((moms, vectors, 2 * vectors), f32),
            pltpu.VMEM((moms, vectors, 2 * vectors), bf16),
            pltpu.VMEM((moms, hrows, 2 * vectors), bf16),
            pltpu.VMEM((moms, hrows, 2 * vectors), f32),
            pltpu.VMEM((moms, hrows, 2 * vectors), bf16),
            pltpu.VMEM((others, moms, prows, 2 * vectors), bf16),
            dma((moms,)), dma((moms,)),
            dma((moms, others)), dma((moms, others)),
            dma((moms, others)), dma((moms, others)),
            dma((moms,)), dma((moms,)),
            dma((moms, 2)), dma((moms, 2)),
            dma((pairs, others)), dma((pairs, others)),
            dma((pairs,)), dma((pairs,)),
            dma((pairs, others)), dma((pairs, others)),
            dma((pairs,)),
            dma,
            dma((pairs,)),
        ],
        compiler_params=pltpu.CompilerParams(
            collective_id=0, has_side_effects=True, vmem_limit_bytes=60 << 20
        ),
        name="exchange",
    )(momenta, pair_list, eigvecs, panels)


def local_kernels(eigvecs, momenta, pair_list, panels):
    spins = panels.shape[3] // eigvecs.shape[4]
    return exchange(eigvecs, momenta, pair_list.T, panels, spins)


def phased_block(cosine, sine_part, real_part, imag_part):
    cos_col = cosine[:, None]
    sin_col = sine_part[:, None]
    wave_re = cos_col * real_part + sin_col * imag_part
    wave_im = cos_col * imag_part - sin_col * real_part
    upper = jnp.concatenate([wave_re, wave_im], -1)
    lower = jnp.concatenate([wave_im, -wave_re], -1)
    return jnp.stack([upper, lower], -4).astype(jnp.bfloat16)


def local_general(eigvecs, momenta, pair_list, panels):
    slice_count, _, colors, slab_sites, vectors = eigvecs.shape
    mom_count = momenta.shape[0]
    space_count = lax.axis_size("space")
    cosine, sine_part = phase_table(momenta, lax.axis_index("space") * slab_sites, slab_sites)
    factor = 1.0 / math.sqrt(6.0 * slab_sites * space_count * vectors)
    real_part = eigvecs[:, 0].astype(jnp.float32)
    imag_part = eigvecs[:, 1].astype(jnp.float32)
    phased_all = jnp.concatenate(
        [
            phased_block(cosine[moment], sine_part[moment], real_part, imag_part)
            for moment in range(mom_count)
        ],
        -1,
    )
    phased_all = phased_all.reshape(slice_count, 2, colors, slab_sites, mom_count, 2 * vectors)
    gram_local = jnp.einsum(
        "trcsk,trcsml->tmkl", eigvecs, phased_all, preferred_element_type=jnp.float32
    )
    gram_local = factor * gram_local
    summed = lax.psum(gram_local, "space")
    own_fields = summed.astype(jnp.bfloat16)
    meson_fields = lax.all_gather(own_fields, "tm", axis=0, tiled=True)
    pair_count = pair_list.shape[0]
    panel_rows = panels.shape[2]
    panel_width = panels.shape[3]
    spins = panel_width // vectors
    source_fields = jnp.take(meson_fields, pair_list[:, 0], axis=0).reshape(
        pair_count, mom_count, vectors, 2, vectors
    )
    sink_fields = jnp.take(meson_fields, pair_list[:, 1], axis=0).reshape(
        pair_count, mom_count, vectors, 2, vectors
    )
    panel_parts = panels.reshape(pair_count, 2, panel_rows, spins, vectors)
    panel_re = panel_parts[:, 0]
    panel_im = panel_parts[:, 1]
    panel_mix = jnp.stack(
        [jnp.stack([panel_re, panel_im], 1), jnp.stack([panel_im, -panel_re], 1)], 1
    )
    right_dressed = jnp.einsum(
        "porxbk,pmlrk->pmoxbl", panel_mix, source_fields, preferred_element_type=jnp.float32
    )
    right_dressed = right_dressed.astype(jnp.bfloat16).reshape(
        pair_count * mom_count, 2, panel_rows, panel_width
    )
    turned = lax.all_to_all(right_dressed, "space", split_axis=3, concat_axis=2, tiled=True)
    column_count = turned.shape[3]
    turned = turned.reshape(pair_count, mom_count, 2, spins, vectors, column_count)
    turned_re = turned[:, :, 0]
    turned_im = turned[:, :, 1]
    mixed_parts = jnp.stack(
        [jnp.stack([turned_re, -turned_im], 2), jnp.stack([turned_im, turned_re], 2)], 2
    )
    dressed = jnp.einsum(
        "pmorajc,pmkrj->pmocak", mixed_parts, sink_fields, preferred_element_type=jnp.float32
    )
    return dressed.reshape(pair_count, mom_count, 2, column_count, panel_width).astype(jnp.bfloat16)


def local(eigvecs, momenta, pair_list, panels):
    slices, _, _, _, vectors = eigvecs.shape
    spins = panels.shape[3] // vectors
    fits = (
        slices == 1
        and lax.axis_size("tm") == 2
        and lax.axis_size("space") == 2 * spins
        and spins > 1
        and spins & (spins - 1) == 0
        and LX & (LX - 1) == 0
        and momenta.shape[0] <= 128
        and panels.shape[2] * 2 == vectors
        and panels.shape[2] % 128 == 0
        and (vectors // 2) % (16 * spins) == 0
    )
    return (local_kernels if fits else local_general)(eigvecs, momenta, pair_list, panels)


def solution(mesh):
    placed = (
        P(("cfg", "tm"), None, None, "space", None),
        P(),
        P("tm", None),
        P(("cfg", "tm"), None, "space", None),
    )
    return jax.shard_map(
        local,
        mesh=mesh,
        in_specs=placed,
        out_specs=P(("cfg", "tm"), None, None, "space", None),
        check_vma=False,
    )
```

```python
import functools
import math

import jax
import jax.numpy as jnp
from jax import lax
from jax.experimental import pallas as pl
from jax.experimental.pallas import tpu as pltpu
from jax.sharding import PartitionSpec as P

LX = 64
MESH = pl.DeviceIdType.MESH


def phase_table(momenta, first_site, slab_sites):
    site_index = first_site + jnp.arange(slab_sites, dtype=jnp.int32)
    xpos = site_index % LX
    ypos = site_index // LX % LX
    zpos = site_index // (LX * LX)
    wave = (
        momenta[:, 0:1] * xpos[None, :]
        + momenta[:, 1:2] * ypos[None, :]
        + momenta[:, 2:3] * zpos[None, :]
    )
    wave = jnp.mod(wave, LX)
    angle = wave.astype(jnp.float32) * jnp.float32(2.0 * math.pi / LX)
    return jnp.cos(angle), jnp.sin(angle)


def products(from_first, to_first, half, tau, mes, made, left, right, sink):
    moms, vectors = mes.shape[1], mes.shape[2]
    spins = tau.shape[1] // vectors
    cols = vectors // 2
    turned = (((1,), (1,)), ((), ()))
    for m in range(moms):
        field = jnp.where(from_first, mes[0, m, half, :], mes[1, m, half, :])
        real_part = field[:, :vectors]
        imag_part = field[:, vectors:]
        left[pl.ds(2 * m * cols, cols), :vectors] = real_part
        left[pl.ds(2 * m * cols, cols), vectors:] = imag_part
        left[pl.ds((2 * m + 1) * cols, cols), :vectors] = -imag_part
        left[pl.ds((2 * m + 1) * cols, cols), vectors:] = real_part
    for spin in range(spins):
        rows = pl.ds(spin * vectors, vectors)
        value = lax.dot_general(
            left[:, :vectors], tau[0, rows, :], turned, preferred_element_type=jnp.float32
        ) + lax.dot_general(
            left[:, vectors:], tau[1, rows, :], turned, preferred_element_type=jnp.float32
        )
        value = value.astype(jnp.bfloat16)
        for m in range(moms):
            for o in range(2):
                right[m, pl.ds(spin * cols, cols), o * vectors : (o + 1) * vectors] = value[
                    (2 * m + o) * cols : (2 * m + o + 1) * cols
                ]
    for m in range(moms):
        field = jnp.where(to_first, mes[0, m], mes[1, m])
        real_part = field[:, :vectors]
        imag_part = field[:, vectors:]
        sink[:vectors, :vectors] = real_part
        sink[:vectors, vectors:] = -imag_part
        sink[vectors:, :vectors] = imag_part
        sink[vectors:, vectors:] = real_part
        value = lax.dot_general(
            right[m], sink[...], turned, preferred_element_type=jnp.float32
        ).astype(jnp.bfloat16)
        for spin in range(spins):
            for o in range(2):
                made[m, o, :, pl.ds(spin * vectors, vectors)] = value[
                    spin * cols : (spin + 1) * cols, o * vectors : (o + 1) * vectors
                ]


def finish_kernel(pair_list, side, done, tau, mes, out, made, left, right, sink, s_done, s_made):
    last = out.shape[0] - 1
    cols = mes.shape[2] // 2
    copy = pltpu.make_async_copy(done, out.at[pl.ds(0, last)], s_done)
    copy.start()
    products(
        pair_list[0, last] == 0, pair_list[1, last] == 0,
        pl.ds(pl.multiple_of(side[0] * cols, cols), cols), tau, mes, made, left, right, sink,
    )
    ending = pltpu.make_async_copy(made, out.at[last], s_made)
    ending.start()
    copy.wait()
    ending.wait()


def finish(pair_list, side, done, tau, mes):
    last, moms, _, cols, width = done.shape
    vectors = mes.shape[2]
    bf16 = jnp.bfloat16
    smem = pl.BlockSpec(memory_space=pltpu.SMEM)
    vmem = pl.BlockSpec(memory_space=pltpu.VMEM)
    hbm = pl.BlockSpec(memory_space=pl.ANY)
    return pl.pallas_call(
        finish_kernel,
        out_shape=jax.ShapeDtypeStruct((last + 1,) + done.shape[1:], bf16),
        in_specs=[smem, smem, hbm, vmem, vmem],
        out_specs=hbm,
        scratch_shapes=[
            pltpu.VMEM((moms, 2, cols, width), bf16),
            pltpu.VMEM((2 * moms * cols, 2 * vectors), bf16),
            pltpu.VMEM((moms, width // vectors * cols, 2 * vectors), bf16),
            pltpu.VMEM((2 * vectors, 2 * vectors), bf16),
            pltpu.SemaphoreType.DMA,
            pltpu.SemaphoreType.DMA,
        ],
        compiler_params=pltpu.CompilerParams(vmem_limit_bytes=16 << 20),
        name="finish",
    )(pair_list, side, done, tau, mes)


def exchange_kernel(
    factor, blocks, momenta, pair_list, eig_hbm, pan, out, tau_last, mes_out,
    tau, mes, left, right, sink, made, eig, stack, wave, gram, part, got,
    s_sum, r_sum, s_field, r_field,
    s_core, r_core, s_pan, r_pan, s_own, r_own, s_fwd, r_fwd, s_loc, s_eig, s_out, s_mes,
):
    space = lax.axis_index("space")
    core = lax.axis_index("tm")
    block = space // 2
    side = space % 2
    other_side = block * 2 + (1 - side)
    pairs, _, rows, _ = pan.shape
    moms, vectors, _ = gram.shape
    colors, sites = eig.shape[1], eig.shape[2]
    hrows = vectors // 2

    fetch = pltpu.make_async_copy(eig_hbm.at[0], eig, s_eig)
    fetch.start()

    def peer(step):
        index, bit = block, 1
        while bit < blocks:
            if (blocks - step) & bit:
                index = index + bit * (1 - 2 * ((block // bit) % 2))
            bit *= 2
        return index

    sender = peer

    def at(index):
        return {"space": index}

    barrier = pltpu.get_barrier_semaphore()
    for step in range(1, blocks):
        pl.semaphore_signal(
            barrier, inc=1, device_id=at(peer(step) * 2 + side), device_id_type=MESH
        )
    pl.semaphore_signal(barrier, inc=1, device_id=at(other_side), device_id_type=MESH)
    pl.semaphore_signal(barrier, inc=1, device_id={"tm": 1 - core}, device_id_type=MESH)
    pl.semaphore_wait(barrier, blocks + 1)

    def remote(src, dst, send, recv, device):
        return pltpu.make_async_remote_copy(
            src_ref=src, dst_ref=dst, send_sem=send, recv_sem=recv,
            device_id=device, device_id_type=MESH,
        )

    def tau_rows(p, owner):
        whole = tau_last if p == pairs - 1 else tau.at[p]
        return whole.at[:, pl.ds(pl.multiple_of(owner * rows, rows), rows), :]

    def pan_cols(index):
        return pl.ds(pl.multiple_of(index * vectors, vectors), vectors)

    along = [
        [
            remote(
                pan.at[p, :, :, pan_cols(peer(step))], tau_rows(p, space),
                s_pan.at[p, step - 1], r_pan.at[p, step - 1], at(peer(step) * 2 + side),
            )
            for step in range(1, blocks)
        ]
        for p in range(pairs)
    ]
    own = [
        remote(
            pan.at[p, :, :, pan_cols(block)], tau_rows(p, space),
            s_own.at[p], r_own.at[p], at(other_side),
        )
        for p in range(pairs)
    ]
    keep = [
        pltpu.make_async_copy(
            pan.at[p, :, :, pan_cols(block)], tau_rows(p, space), s_loc.at[p]
        )
        for p in range(pairs)
    ]
    forward = [
        [
            remote(
                tau_rows(p, sender(step) * 2 + side),
                tau_rows(p, sender(step) * 2 + side),
                s_fwd.at[p, step - 1], r_fwd.at[p, step - 1], at(other_side),
            )
            for step in range(1, blocks)
        ]
        for p in range(pairs)
    ]
    my_half = pl.ds(pl.multiple_of(side * hrows, hrows), hrows)
    steps = []
    size, base, landing, bit = vectors, 0, 0, 1
    while bit < blocks:
        own_bit = (block // bit) % 2
        kinds = [(own_bit, (block + bit * (1 - 2 * own_bit)) * 2 + side)]
        if bit == 1:
            kinds.append((side, other_side))
        for mine, partner in kinds:
            size //= 2
            near = pl.ds(pl.multiple_of(base + mine * size, size), size)
            far = pl.ds(pl.multiple_of(base + (1 - mine) * size, size), size)
            steps.append((partner, near, far, pl.ds(landing, size)))
            base = base + mine * size
            landing += size
        bit *= 2
    sums = [
        [
            remote(
                part.at[m, far, :], got.at[m, land, :],
                s_sum.at[k, m], r_sum.at[k, m], at(partner),
            )
            for m in range(moms)
        ]
        for k, (partner, near, far, land) in enumerate(steps)
    ]
    fields = [
        [
            remote(
                mes.at[core, m, near, :], mes.at[core, m, near, :],
                s_field.at[k, m], r_field.at[k, m], at(partner),
            )
            for m in range(moms)
        ]
        for k, (partner, near, far, land) in enumerate(steps)
    ]
    cores = [
        [
            remote(
                mes.at[core, m, which, :], mes.at[core, m, which, :],
                s_core.at[m, i], r_core.at[m, i], {"tm": 1 - core},
            )
            for i, which in enumerate(steps[0][1:3])
        ]
        for m in range(moms)
    ]

    def send_along(p):
        for copy in along[p]:
            copy.start()

    def pass_on(p):
        for step in range(blocks - 1):
            along[p][step].wait_recv()
            forward[p][step].start()

    put = [pltpu.make_async_copy(made.at[p], out.at[p], s_out.at[p]) for p in range(pairs - 1)]

    def dress(p):
        products(
            pair_list[0, p] == 0, pair_list[1, p] == 0, my_half, tau.at[p], mes, made.at[p],
            left, right, sink,
        )
        put[p].start()

    def settle(p):
        keep[p].wait()
        own[p].wait_recv()
        for copy in forward[p]:
            copy.wait_recv()

    send_along(0)
    own[0].start()
    for copy in keep:
        copy.start()

    site = space * sites + lax.broadcasted_iota(jnp.int32, (sites, 128), 0)
    lane = lax.broadcasted_iota(jnp.int32, (sites, 128), 1)
    turn = jnp.zeros((sites, 128), jnp.int32)
    shift = LX.bit_length() - 1
    for m in range(moms):
        sum_m = (
            momenta[m, 0] * (site & (LX - 1))
            + momenta[m, 1] * (lax.shift_right_logical(site, shift) & (LX - 1))
            + momenta[m, 2] * lax.shift_right_logical(site, 2 * shift)
        )
        turn = jnp.where(lane == m, sum_m & (LX - 1), turn)
    angle = turn.astype(jnp.float32) * jnp.float32(2.0 * math.pi / LX)
    cosine = jnp.cos(angle)
    sine = jnp.sin(angle)
    fetch.wait()
    for color in range(colors):
        for r in range(2):
            stack[pl.ds((r * colors + color) * sites, sites), :] = eig[r, color]
    for m in range(moms):
        cos_col = cosine[:, m : m + 1]
        sin_col = sine[:, m : m + 1]
        for color in range(colors):
            real_part = eig[0, color].astype(jnp.float32)
            imag_part = eig[1, color].astype(jnp.float32)
            wave_re = (cos_col * real_part + sin_col * imag_part).astype(jnp.bfloat16)
            wave_im = (cos_col * imag_part - sin_col * real_part).astype(jnp.bfloat16)
            upper = pl.ds(color * sites, sites)
            lower = pl.ds((colors + color) * sites, sites)
            wave[upper, :vectors] = wave_re
            wave[upper, vectors:] = wave_im
            wave[lower, :vectors] = wave_im
            wave[lower, vectors:] = -wave_re
        total = factor * lax.dot_general(
            stack[...], wave[...], (((0,), (0,)), ((), ())), preferred_element_type=jnp.float32
        )
        gram[m] = total
        part[m] = total.astype(jnp.bfloat16)
        sums[0][m].start()

    def add_up(k):
        _, near, _, land = steps[k]
        for m in range(moms):
            sums[k][m].wait_recv()
            value = gram[m, near, :] + got[m, land, :].astype(jnp.float32)
            if k + 1 < len(steps):
                gram[m, near, :] = value
                part[m, near, :] = value.astype(jnp.bfloat16)
                sums[k + 1][m].start()
            else:
                mes[core, m, near, :] = value.astype(jnp.bfloat16)
                fields[k][m].start()

    send_along(1)
    add_up(0)
    for p in range(1, pairs):
        own[p].start()
    pass_on(0)
    for k in range(1, len(steps)):
        add_up(k)
    send_along(2)
    pass_on(1)
    for k in reversed(range(1, len(steps))):
        for m in range(moms):
            fields[k][m].wait_recv()
            fields[k - 1][m].start()
            if k == 1:
                cores[m][0].start()
    for p in range(3, pairs):
        send_along(p)
    for p in range(2, pairs - 1):
        pass_on(p)
    for m in range(moms):
        fields[0][m].wait_recv()
        cores[m][1].start()
    for m in range(moms):
        for copy in cores[m]:
            copy.wait_recv()
    keep_mes = pltpu.make_async_copy(mes, mes_out, s_mes)
    keep_mes.start()
    last = pairs - 1
    for p in range(last):
        settle(p)
        dress(p)
        if p < blocks - 1:
            along[last][p].wait_recv()
            forward[last][p].start()
    for step in range(last, blocks - 1):
        along[last][step].wait_recv()
        forward[last][step].start()
    settle(last)

    for m in range(moms):
        for k in range(len(steps)):
            sums[k][m].wait_send()
            fields[k][m].wait_send()
        for copy in cores[m]:
            copy.wait_send()
    for p in range(pairs):
        own[p].wait_send()
        for copy in along[p] + forward[p]:
            copy.wait_send()
    for copy in put:
        copy.wait()
    keep_mes.wait()


def exchange(eigvecs, momenta, pair_list, panels, spins):
    pairs, _, rows, width = panels.shape
    _, _, colors, sites, vectors = eigvecs.shape
    moms = momenta.shape[0]
    space_count = lax.axis_size("space")
    slices = lax.axis_size("tm")
    factor = 1.0 / math.sqrt(6.0 * sites * space_count * vectors)
    hrows = vectors // 2
    steps = spins.bit_length()
    bf16, f32 = jnp.bfloat16, jnp.float32
    dma = pltpu.SemaphoreType.DMA
    others = spins - 1
    smem = pl.BlockSpec(memory_space=pltpu.SMEM)
    hbm = pl.BlockSpec(memory_space=pltpu.HBM)
    anywhere = pl.BlockSpec(memory_space=pl.ANY)
    return pl.pallas_call(
        functools.partial(exchange_kernel, factor, spins),
        out_shape=(
            jax.ShapeDtypeStruct((pairs - 1, moms, 2, rows, width), bf16),
            jax.ShapeDtypeStruct((2, rows * space_count, vectors), bf16),
            jax.ShapeDtypeStruct((slices, moms, vectors, 2 * vectors), bf16),
        ),
        in_specs=[smem, smem, hbm, hbm],
        out_specs=(anywhere,) * 3,
        scratch_shapes=[
            pltpu.VMEM((pairs - 1, 2, rows * space_count, vectors), bf16),
            pltpu.VMEM((slices, moms, vectors, 2 * vectors), bf16),
            pltpu.VMEM((2 * moms * hrows, 2 * vectors), bf16),
            pltpu.VMEM((moms, spins * hrows, 2 * vectors), bf16),
            pltpu.VMEM((2 * vectors, 2 * vectors), bf16),
            pltpu.VMEM((pairs - 1, moms, 2, rows, width), bf16),
            pltpu.VMEM((2, colors, sites, vectors), bf16),
            pltpu.VMEM((2 * colors * sites, vectors), bf16),
            pltpu.VMEM((2 * colors * sites, 2 * vectors), bf16),
            pltpu.VMEM((moms, vectors, 2 * vectors), f32),
            pltpu.VMEM((moms, vectors, 2 * vectors), bf16),
            pltpu.VMEM((moms, vectors, 2 * vectors), bf16),
            dma((steps, moms)), dma((steps, moms)),
            dma((steps, moms)), dma((steps, moms)),
            dma((moms, 2)), dma((moms, 2)),
            dma((pairs, others)), dma((pairs, others)),
            dma((pairs,)), dma((pairs,)),
            dma((pairs, others)), dma((pairs, others)),
            dma((pairs,)),
            dma,
            dma((pairs - 1,)),
            dma,
        ],
        compiler_params=pltpu.CompilerParams(
            collective_id=0, has_side_effects=True, vmem_limit_bytes=36 << 20
        ),
        name="exchange",
    )(momenta, pair_list, eigvecs, panels)


def local_kernels(eigvecs, momenta, pair_list, panels):
    spins = panels.shape[3] // eigvecs.shape[4]
    done, tau, mes = exchange(eigvecs, momenta, pair_list.T, panels, spins)
    side = jnp.reshape(lax.axis_index("space") % 2, (1,)).astype(jnp.int32)
    return finish(pair_list.T, side, done, tau, mes)


def phased_block(cosine, sine_part, real_part, imag_part):
    cos_col = cosine[:, None]
    sin_col = sine_part[:, None]
    wave_re = cos_col * real_part + sin_col * imag_part
    wave_im = cos_col * imag_part - sin_col * real_part
    upper = jnp.concatenate([wave_re, wave_im], -1)
    lower = jnp.concatenate([wave_im, -wave_re], -1)
    return jnp.stack([upper, lower], -4).astype(jnp.bfloat16)


def local_general(eigvecs, momenta, pair_list, panels):
    slice_count, _, colors, slab_sites, vectors = eigvecs.shape
    mom_count = momenta.shape[0]
    space_count = lax.axis_size("space")
    cosine, sine_part = phase_table(momenta, lax.axis_index("space") * slab_sites, slab_sites)
    factor = 1.0 / math.sqrt(6.0 * slab_sites * space_count * vectors)
    real_part = eigvecs[:, 0].astype(jnp.float32)
    imag_part = eigvecs[:, 1].astype(jnp.float32)
    phased_all = jnp.concatenate(
        [
            phased_block(cosine[moment], sine_part[moment], real_part, imag_part)
            for moment in range(mom_count)
        ],
        -1,
    )
    phased_all = phased_all.reshape(slice_count, 2, colors, slab_sites, mom_count, 2 * vectors)
    gram_local = jnp.einsum(
        "trcsk,trcsml->tmkl", eigvecs, phased_all, preferred_element_type=jnp.float32
    )
    gram_local = factor * gram_local
    summed = lax.psum(gram_local, "space")
    own_fields = summed.astype(jnp.bfloat16)
    meson_fields = lax.all_gather(own_fields, "tm", axis=0, tiled=True)
    pair_count = pair_list.shape[0]
    panel_rows = panels.shape[2]
    panel_width = panels.shape[3]
    spins = panel_width // vectors
    source_fields = jnp.take(meson_fields, pair_list[:, 0], axis=0).reshape(
        pair_count, mom_count, vectors, 2, vectors
    )
    sink_fields = jnp.take(meson_fields, pair_list[:, 1], axis=0).reshape(
        pair_count, mom_count, vectors, 2, vectors
    )
    panel_parts = panels.reshape(pair_count, 2, panel_rows, spins, vectors)
    panel_re = panel_parts[:, 0]
    panel_im = panel_parts[:, 1]
    panel_mix = jnp.stack(
        [jnp.stack([panel_re, panel_im], 1), jnp.stack([panel_im, -panel_re], 1)], 1
    )
    right_dressed = jnp.einsum(
        "porxbk,pmlrk->pmoxbl", panel_mix, source_fields, preferred_element_type=jnp.float32
    )
    right_dressed = right_dressed.astype(jnp.bfloat16).reshape(
        pair_count * mom_count, 2, panel_rows, panel_width
    )
    turned = lax.all_to_all(right_dressed, "space", split_axis=3, concat_axis=2, tiled=True)
    column_count = turned.shape[3]
    turned = turned.reshape(pair_count, mom_count, 2, spins, vectors, column_count)
    turned_re = turned[:, :, 0]
    turned_im = turned[:, :, 1]
    mixed_parts = jnp.stack(
        [jnp.stack([turned_re, -turned_im], 2), jnp.stack([turned_im, turned_re], 2)], 2
    )
    dressed = jnp.einsum(
        "pmorajc,pmkrj->pmocak", mixed_parts, sink_fields, preferred_element_type=jnp.float32
    )
    return dressed.reshape(pair_count, mom_count, 2, column_count, panel_width).astype(jnp.bfloat16)


def local(eigvecs, momenta, pair_list, panels):
    slices, _, _, _, vectors = eigvecs.shape
    spins = panels.shape[3] // vectors
    fits = (
        slices == 1
        and lax.axis_size("tm") == 2
        and lax.axis_size("space") == 2 * spins
        and spins > 1
        and spins & (spins - 1) == 0
        and LX & (LX - 1) == 0
        and momenta.shape[0] <= 128
        and pair_list.shape[0] > 2
        and panels.shape[2] * 2 == vectors
        and panels.shape[2] % 128 == 0
        and (vectors // 2) % (16 * spins) == 0
    )
    return (local_kernels if fits else local_general)(eigvecs, momenta, pair_list, panels)


def solution(mesh):
    placed = (
        P(("cfg", "tm"), None, None, "space", None),
        P(),
        P("tm", None),
        P(("cfg", "tm"), None, "space", None),
    )
    return jax.shard_map(
        local,
        mesh=mesh,
        in_specs=placed,
        out_specs=P(("cfg", "tm"), None, None, "space", None),
        check_vma=False,
    )
```

```python
import functools
import math

import jax
import jax.numpy as jnp
from jax import lax
from jax.experimental import pallas as pl
from jax.experimental.pallas import tpu as pltpu
from jax.sharding import PartitionSpec as P

LX = 64
MESH = pl.DeviceIdType.MESH


def phase_table(momenta, first_site, slab_sites):
    site_index = first_site + jnp.arange(slab_sites, dtype=jnp.int32)
    xpos = site_index % LX
    ypos = site_index // LX % LX
    zpos = site_index // (LX * LX)
    wave = (
        momenta[:, 0:1] * xpos[None, :]
        + momenta[:, 1:2] * ypos[None, :]
        + momenta[:, 2:3] * zpos[None, :]
    )
    wave = jnp.mod(wave, LX)
    angle = wave.astype(jnp.float32) * jnp.float32(2.0 * math.pi / LX)
    return jnp.cos(angle), jnp.sin(angle)


def products(from_first, to_first, half, tau, mes, made, left, right, sink):
    moms, vectors = mes.shape[1], mes.shape[2]
    spins = tau.shape[1] // vectors
    cols = vectors // 2
    turned = (((1,), (1,)), ((), ()))
    for m in range(moms):
        field = jnp.where(from_first, mes[0, m, half, :], mes[1, m, half, :])
        real_part = field[:, :vectors]
        imag_part = field[:, vectors:]
        left[pl.ds(2 * m * cols, cols), :vectors] = real_part
        left[pl.ds(2 * m * cols, cols), vectors:] = imag_part
        left[pl.ds((2 * m + 1) * cols, cols), :vectors] = -imag_part
        left[pl.ds((2 * m + 1) * cols, cols), vectors:] = real_part
    for spin in range(spins):
        rows = pl.ds(spin * vectors, vectors)
        value = lax.dot_general(
            left[:, :vectors], tau[0, rows, :], turned, preferred_element_type=jnp.float32
        ) + lax.dot_general(
            left[:, vectors:], tau[1, rows, :], turned, preferred_element_type=jnp.float32
        )
        value = value.astype(jnp.bfloat16)
        for m in range(moms):
            for o in range(2):
                right[m, pl.ds(spin * cols, cols), o * vectors : (o + 1) * vectors] = value[
                    (2 * m + o) * cols : (2 * m + o + 1) * cols
                ]
    for m in range(moms):
        field = jnp.where(to_first, mes[0, m], mes[1, m])
        real_part = field[:, :vectors]
        imag_part = field[:, vectors:]
        sink[:vectors, :vectors] = real_part
        sink[:vectors, vectors:] = -imag_part
        sink[vectors:, :vectors] = imag_part
        sink[vectors:, vectors:] = real_part
        value = lax.dot_general(
            right[m], sink[...], turned, preferred_element_type=jnp.float32
        ).astype(jnp.bfloat16)
        for spin in range(spins):
            for o in range(2):
                made[m, o, :, pl.ds(spin * vectors, vectors)] = value[
                    spin * cols : (spin + 1) * cols, o * vectors : (o + 1) * vectors
                ]


def finish_kernel(pair_list, side, done, tau, mes, out, made, left, right, sink, s_done, s_made):
    last = out.shape[0] - 1
    cols = mes.shape[2] // 2
    copy = pltpu.make_async_copy(done, out.at[pl.ds(0, last)], s_done)
    copy.start()
    products(
        pair_list[0, last] == 0, pair_list[1, last] == 0,
        pl.ds(pl.multiple_of(side[0] * cols, cols), cols), tau, mes, made, left, right, sink,
    )
    ending = pltpu.make_async_copy(made, out.at[last], s_made)
    ending.start()
    copy.wait()
    ending.wait()


def finish(pair_list, side, done, tau, mes):
    last, moms, _, cols, width = done.shape
    vectors = mes.shape[2]
    bf16 = jnp.bfloat16
    smem = pl.BlockSpec(memory_space=pltpu.SMEM)
    vmem = pl.BlockSpec(memory_space=pltpu.VMEM)
    hbm = pl.BlockSpec(memory_space=pl.ANY)
    return pl.pallas_call(
        finish_kernel,
        out_shape=jax.ShapeDtypeStruct((last + 1,) + done.shape[1:], bf16),
        in_specs=[smem, smem, hbm, vmem, vmem],
        out_specs=hbm,
        scratch_shapes=[
            pltpu.VMEM((moms, 2, cols, width), bf16),
            pltpu.VMEM((2 * moms * cols, 2 * vectors), bf16),
            pltpu.VMEM((moms, width // vectors * cols, 2 * vectors), bf16),
            pltpu.VMEM((2 * vectors, 2 * vectors), bf16),
            pltpu.SemaphoreType.DMA,
            pltpu.SemaphoreType.DMA,
        ],
        compiler_params=pltpu.CompilerParams(vmem_limit_bytes=16 << 20),
        name="finish",
    )(pair_list, side, done, tau, mes)


def exchange_kernel(
    factor, blocks, momenta, pair_list, eig_hbm, pan, out, tau_last, mes_out,
    tau, mes, left, right, sink, made, eig, stack, wave, gram, part, got,
    s_sum, r_sum, s_field, r_field,
    s_core, r_core, s_pan, r_pan, s_own, r_own, s_fwd, r_fwd, s_loc, s_eig, s_out, s_mes,
):
    space = lax.axis_index("space")
    core = lax.axis_index("tm")
    block = space // 2
    side = space % 2
    other_side = block * 2 + (1 - side)
    pairs, _, rows, _ = pan.shape
    moms, vectors, _ = gram.shape
    colors, sites = eig.shape[1], eig.shape[2]
    hrows = vectors // 2

    fetch = pltpu.make_async_copy(eig_hbm.at[0], eig, s_eig)
    fetch.start()

    def peer(step):
        index, bit = block, 1
        while bit < blocks:
            if (blocks - step) & bit:
                index = index + bit * (1 - 2 * ((block // bit) % 2))
            bit *= 2
        return index

    sender = peer

    def at(index):
        return {"space": index}

    barrier = pltpu.get_barrier_semaphore()
    for step in range(1, blocks):
        pl.semaphore_signal(
            barrier, inc=1, device_id=at(peer(step) * 2 + side), device_id_type=MESH
        )
    pl.semaphore_signal(barrier, inc=1, device_id=at(other_side), device_id_type=MESH)
    pl.semaphore_signal(barrier, inc=1, device_id={"tm": 1 - core}, device_id_type=MESH)
    pl.semaphore_wait(barrier, blocks + 1)

    def remote(src, dst, send, recv, device):
        return pltpu.make_async_remote_copy(
            src_ref=src, dst_ref=dst, send_sem=send, recv_sem=recv,
            device_id=device, device_id_type=MESH,
        )

    def tau_rows(p, owner):
        whole = tau_last if p == pairs - 1 else tau.at[p]
        return whole.at[:, pl.ds(pl.multiple_of(owner * rows, rows), rows), :]

    def pan_cols(index):
        return pl.ds(pl.multiple_of(index * vectors, vectors), vectors)

    along = [
        [
            remote(
                pan.at[p, :, :, pan_cols(peer(step))], tau_rows(p, space),
                s_pan.at[p, step - 1], r_pan.at[p, step - 1], at(peer(step) * 2 + side),
            )
            for step in range(1, blocks)
        ]
        for p in range(pairs)
    ]
    own = [
        remote(
            pan.at[p, :, :, pan_cols(block)], tau_rows(p, space),
            s_own.at[p], r_own.at[p], at(other_side),
        )
        for p in range(pairs)
    ]
    keep = [
        pltpu.make_async_copy(
            pan.at[p, :, :, pan_cols(block)], tau_rows(p, space), s_loc.at[p]
        )
        for p in range(pairs)
    ]
    forward = [
        [
            remote(
                tau_rows(p, sender(step) * 2 + side),
                tau_rows(p, sender(step) * 2 + side),
                s_fwd.at[p, step - 1], r_fwd.at[p, step - 1], at(other_side),
            )
            for step in range(1, blocks)
        ]
        for p in range(pairs)
    ]
    my_half = pl.ds(pl.multiple_of(side * hrows, hrows), hrows)
    steps = []
    size, base, landing, bit = vectors, 0, 0, 1
    while bit < blocks:
        own_bit = (block // bit) % 2
        kinds = [(own_bit, (block + bit * (1 - 2 * own_bit)) * 2 + side)]
        if bit == 1:
            kinds.append((side, other_side))
        for mine, partner in kinds:
            size //= 2
            near = pl.ds(pl.multiple_of(base + mine * size, size), size)
            far = pl.ds(pl.multiple_of(base + (1 - mine) * size, size), size)
            steps.append((partner, near, far, pl.ds(landing, size)))
            base = base + mine * size
            landing += size
        bit *= 2
    sums = [
        [
            remote(
                part.at[m, far, :], got.at[m, land, :],
                s_sum.at[k, m], r_sum.at[k, m], at(partner),
            )
            for m in range(moms)
        ]
        for k, (partner, near, far, land) in enumerate(steps)
    ]
    fields = [
        [
            remote(
                mes.at[core, m, near, :], mes.at[core, m, near, :],
                s_field.at[k, m], r_field.at[k, m], at(partner),
            )
            for m in range(moms)
        ]
        for k, (partner, near, far, land) in enumerate(steps)
    ]
    cores = [
        [
            remote(
                mes.at[core, m, which, :], mes.at[core, m, which, :],
                s_core.at[m, i], r_core.at[m, i], {"tm": 1 - core},
            )
            for i, which in enumerate(steps[0][1:3])
        ]
        for m in range(moms)
    ]

    def send_along(p):
        for copy in along[p]:
            copy.start()

    def pass_on(p):
        for step in range(blocks - 1):
            along[p][step].wait_recv()
            forward[p][step].start()

    put = [pltpu.make_async_copy(made.at[p], out.at[p], s_out.at[p]) for p in range(pairs - 1)]

    def dress(p):
        products(
            pair_list[0, p] == 0, pair_list[1, p] == 0, my_half, tau.at[p], mes, made.at[p],
            left, right, sink,
        )
        put[p].start()

    def settle(p):
        keep[p].wait()
        own[p].wait_recv()
        for copy in forward[p]:
            copy.wait_recv()

    send_along(0)
    for copy in own:
        copy.start()
    for copy in keep:
        copy.start()

    site = space * sites + lax.broadcasted_iota(jnp.int32, (sites, 128), 0)
    lane = lax.broadcasted_iota(jnp.int32, (sites, 128), 1)
    turn = jnp.zeros((sites, 128), jnp.int32)
    shift = LX.bit_length() - 1
    for m in range(moms):
        sum_m = (
            momenta[m, 0] * (site & (LX - 1))
            + momenta[m, 1] * (lax.shift_right_logical(site, shift) & (LX - 1))
            + momenta[m, 2] * lax.shift_right_logical(site, 2 * shift)
        )
        turn = jnp.where(lane == m, sum_m & (LX - 1), turn)
    angle = turn.astype(jnp.float32) * jnp.float32(2.0 * math.pi / LX)
    cosine = jnp.cos(angle)
    sine = jnp.sin(angle)
    fetch.wait()
    for color in range(colors):
        for r in range(2):
            stack[pl.ds((r * colors + color) * sites, sites), :] = eig[r, color]
    for m in range(moms):
        cos_col = cosine[:, m : m + 1]
        sin_col = sine[:, m : m + 1]
        for color in range(colors):
            real_part = eig[0, color].astype(jnp.float32)
            imag_part = eig[1, color].astype(jnp.float32)
            wave_re = (cos_col * real_part + sin_col * imag_part).astype(jnp.bfloat16)
            wave_im = (cos_col * imag_part - sin_col * real_part).astype(jnp.bfloat16)
            upper = pl.ds(color * sites, sites)
            lower = pl.ds((colors + color) * sites, sites)
            wave[upper, :vectors] = wave_re
            wave[upper, vectors:] = wave_im
            wave[lower, :vectors] = wave_im
            wave[lower, vectors:] = -wave_re
        total = factor * lax.dot_general(
            stack[...], wave[...], (((0,), (0,)), ((), ())), preferred_element_type=jnp.float32
        )
        gram[m] = total
        part[m] = total.astype(jnp.bfloat16)
        sums[0][m].start()

    def add_up(k):
        _, near, _, land = steps[k]
        for m in range(moms):
            sums[k][m].wait_recv()
            value = gram[m, near, :] + got[m, land, :].astype(jnp.float32)
            if k + 1 < len(steps):
                gram[m, near, :] = value
                part[m, near, :] = value.astype(jnp.bfloat16)
                sums[k + 1][m].start()
            else:
                mes[core, m, near, :] = value.astype(jnp.bfloat16)
                fields[k][m].start()

    send_along(1)
    add_up(0)
    pass_on(0)
    for k in range(1, len(steps)):
        add_up(k)
    send_along(2)
    pass_on(1)
    for k in reversed(range(1, len(steps))):
        for m in range(moms):
            fields[k][m].wait_recv()
            fields[k - 1][m].start()
            if k == 1:
                cores[m][0].start()
    for p in range(3, pairs):
        send_along(p)
    for p in range(2, pairs - 1):
        pass_on(p)
    for m in range(moms):
        fields[0][m].wait_recv()
        cores[m][1].start()
    for m in range(moms):
        for copy in cores[m]:
            copy.wait_recv()
    keep_mes = pltpu.make_async_copy(mes, mes_out, s_mes)
    keep_mes.start()
    last = pairs - 1
    for p in range(last):
        settle(p)
        dress(p)
        if p < blocks - 1:
            along[last][p].wait_recv()
            forward[last][p].start()
    for step in range(last, blocks - 1):
        along[last][step].wait_recv()
        forward[last][step].start()
    settle(last)

    for m in range(moms):
        for k in range(len(steps)):
            sums[k][m].wait_send()
            fields[k][m].wait_send()
        for copy in cores[m]:
            copy.wait_send()
    for p in range(pairs):
        own[p].wait_send()
        for copy in along[p] + forward[p]:
            copy.wait_send()
    for copy in put:
        copy.wait()
    keep_mes.wait()


def exchange(eigvecs, momenta, pair_list, panels, spins):
    pairs, _, rows, width = panels.shape
    _, _, colors, sites, vectors = eigvecs.shape
    moms = momenta.shape[0]
    space_count = lax.axis_size("space")
    slices = lax.axis_size("tm")
    factor = 1.0 / math.sqrt(6.0 * sites * space_count * vectors)
    hrows = vectors // 2
    steps = spins.bit_length()
    bf16, f32 = jnp.bfloat16, jnp.float32
    dma = pltpu.SemaphoreType.DMA
    others = spins - 1
    smem = pl.BlockSpec(memory_space=pltpu.SMEM)
    hbm = pl.BlockSpec(memory_space=pltpu.HBM)
    anywhere = pl.BlockSpec(memory_space=pl.ANY)
    return pl.pallas_call(
        functools.partial(exchange_kernel, factor, spins),
        out_shape=(
            jax.ShapeDtypeStruct((pairs - 1, moms, 2, rows, width), bf16),
            jax.ShapeDtypeStruct((2, rows * space_count, vectors), bf16),
            jax.ShapeDtypeStruct((slices, moms, vectors, 2 * vectors), bf16),
        ),
        in_specs=[smem, smem, hbm, hbm],
        out_specs=(anywhere,) * 3,
        scratch_shapes=[
            pltpu.VMEM((pairs - 1, 2, rows * space_count, vectors), bf16),
            pltpu.VMEM((slices, moms, vectors, 2 * vectors), bf16),
            pltpu.VMEM((2 * moms * hrows, 2 * vectors), bf16),
            pltpu.VMEM((moms, spins * hrows, 2 * vectors), bf16),
            pltpu.VMEM((2 * vectors, 2 * vectors), bf16),
            pltpu.VMEM((pairs - 1, moms, 2, rows, width), bf16),
            pltpu.VMEM((2, colors, sites, vectors), bf16),
            pltpu.VMEM((2 * colors * sites, vectors), bf16),
            pltpu.VMEM((2 * colors * sites, 2 * vectors), bf16),
            pltpu.VMEM((moms, vectors, 2 * vectors), f32),
            pltpu.VMEM((moms, vectors, 2 * vectors), bf16),
            pltpu.VMEM((moms, vectors, 2 * vectors), bf16),
            dma((steps, moms)), dma((steps, moms)),
            dma((steps, moms)), dma((steps, moms)),
            dma((moms, 2)), dma((moms, 2)),
            dma((pairs, others)), dma((pairs, others)),
            dma((pairs,)), dma((pairs,)),
            dma((pairs, others)), dma((pairs, others)),
            dma((pairs,)),
            dma,
            dma((pairs - 1,)),
            dma,
        ],
        compiler_params=pltpu.CompilerParams(
            collective_id=0, has_side_effects=True, vmem_limit_bytes=36 << 20
        ),
        name="exchange",
    )(momenta, pair_list, eigvecs, panels)


def local_kernels(eigvecs, momenta, pair_list, panels):
    spins = panels.shape[3] // eigvecs.shape[4]
    done, tau, mes = exchange(eigvecs, momenta, pair_list.T, panels, spins)
    side = jnp.reshape(lax.axis_index("space") % 2, (1,)).astype(jnp.int32)
    return finish(pair_list.T, side, done, tau, mes)


def phased_block(cosine, sine_part, real_part, imag_part):
    cos_col = cosine[:, None]
    sin_col = sine_part[:, None]
    wave_re = cos_col * real_part + sin_col * imag_part
    wave_im = cos_col * imag_part - sin_col * real_part
    upper = jnp.concatenate([wave_re, wave_im], -1)
    lower = jnp.concatenate([wave_im, -wave_re], -1)
    return jnp.stack([upper, lower], -4).astype(jnp.bfloat16)


def local_general(eigvecs, momenta, pair_list, panels):
    slice_count, _, colors, slab_sites, vectors = eigvecs.shape
    mom_count = momenta.shape[0]
    space_count = lax.axis_size("space")
    cosine, sine_part = phase_table(momenta, lax.axis_index("space") * slab_sites, slab_sites)
    factor = 1.0 / math.sqrt(6.0 * slab_sites * space_count * vectors)
    real_part = eigvecs[:, 0].astype(jnp.float32)
    imag_part = eigvecs[:, 1].astype(jnp.float32)
    phased_all = jnp.concatenate(
        [
            phased_block(cosine[moment], sine_part[moment], real_part, imag_part)
            for moment in range(mom_count)
        ],
        -1,
    )
    phased_all = phased_all.reshape(slice_count, 2, colors, slab_sites, mom_count, 2 * vectors)
    gram_local = jnp.einsum(
        "trcsk,trcsml->tmkl", eigvecs, phased_all, preferred_element_type=jnp.float32
    )
    gram_local = factor * gram_local
    summed = lax.psum(gram_local, "space")
    own_fields = summed.astype(jnp.bfloat16)
    meson_fields = lax.all_gather(own_fields, "tm", axis=0, tiled=True)
    pair_count = pair_list.shape[0]
    panel_rows = panels.shape[2]
    panel_width = panels.shape[3]
    spins = panel_width // vectors
    source_fields = jnp.take(meson_fields, pair_list[:, 0], axis=0).reshape(
        pair_count, mom_count, vectors, 2, vectors
    )
    sink_fields = jnp.take(meson_fields, pair_list[:, 1], axis=0).reshape(
        pair_count, mom_count, vectors, 2, vectors
    )
    panel_parts = panels.reshape(pair_count, 2, panel_rows, spins, vectors)
    panel_re = panel_parts[:, 0]
    panel_im = panel_parts[:, 1]
    panel_mix = jnp.stack(
        [jnp.stack([panel_re, panel_im], 1), jnp.stack([panel_im, -panel_re], 1)], 1
    )
    right_dressed = jnp.einsum(
        "porxbk,pmlrk->pmoxbl", panel_mix, source_fields, preferred_element_type=jnp.float32
    )
    right_dressed = right_dressed.astype(jnp.bfloat16).reshape(
        pair_count * mom_count, 2, panel_rows, panel_width
    )
    turned = lax.all_to_all(right_dressed, "space", split_axis=3, concat_axis=2, tiled=True)
    column_count = turned.shape[3]
    turned = turned.reshape(pair_count, mom_count, 2, spins, vectors, column_count)
    turned_re = turned[:, :, 0]
    turned_im = turned[:, :, 1]
    mixed_parts = jnp.stack(
        [jnp.stack([turned_re, -turned_im], 2), jnp.stack([turned_im, turned_re], 2)], 2
    )
    dressed = jnp.einsum(
        "pmorajc,pmkrj->pmocak", mixed_parts, sink_fields, preferred_element_type=jnp.float32
    )
    return dressed.reshape(pair_count, mom_count, 2, column_count, panel_width).astype(jnp.bfloat16)


def local(eigvecs, momenta, pair_list, panels):
    slices, _, _, _, vectors = eigvecs.shape
    spins = panels.shape[3] // vectors
    fits = (
        slices == 1
        and lax.axis_size("tm") == 2
        and lax.axis_size("space") == 2 * spins
        and spins > 1
        and spins & (spins - 1) == 0
        and LX & (LX - 1) == 0
        and momenta.shape[0] <= 128
        and pair_list.shape[0] > 2
        and panels.shape[2] * 2 == vectors
        and panels.shape[2] % 128 == 0
        and (vectors // 2) % (16 * spins) == 0
    )
    return (local_kernels if fits else local_general)(eigvecs, momenta, pair_list, panels)


def solution(mesh):
    placed = (
        P(("cfg", "tm"), None, None, "space", None),
        P(),
        P("tm", None),
        P(("cfg", "tm"), None, "space", None),
    )
    return jax.shard_map(
        local,
        mesh=mesh,
        in_specs=placed,
        out_specs=P(("cfg", "tm"), None, None, "space", None),
        check_vma=False,
    )
```
